32 devices in a mesh: tm: 4 (over x, core), span: 8 (over z, y).
Axes of the slice: x: 2, y: 2, z: 4, core: 2. Of those that a mesh axis runs over, the one named last changes fastest.
Arguments:
- forcing: bfloat16 [128, 8, 16, 128], P('tm', 'span'), may hold values from -1.5 to 1.5
- iterate: bfloat16 [128, 8, 16, 128], P('tm', 'span'), may hold values from -1.5 to 1.5
- initial: bfloat16 [8, 16, 128], P('span'), may hold values from -1.5 to 1.5
- stiffness: bfloat16 [8, 128, 128], P('span'), may hold values from -0.5 to 0.5
- coupling: bfloat16 [8, 128, 128], P('span'), may hold values from -0.5 to 0.5
- pivots: bfloat16 [128, 8, 2, 128, 128], P('tm', 'span'), may hold values from -0.375 to 0.375
Outputs:
- updated: float32 [128, 8, 16, 128], P('tm', 'span')
The draws below stay inside these ranges and needn't reach their ends.
All inputs are finite; a program needn't handle non-finite values.
Results may differ from the reference program's by a relative error of at most 0.0003.
Values may be sent and summed in bfloat16 or wider, within the bound.
A program may use at most 320 MiB of HBM per device.

```python
import math
import jax
import jax.numpy as jnp
from jax import lax

DOF = 128
L = 128
RC = 16
NP = 8


def steps_of(stream_key, dims, cuts, smallest, largest):
    def one(dim, parts):
        steps = jax.random.uniform(jax.random.fold_in(jax.random.fold_in(stream_key, 6), dim), (parts,), jnp.float32, smallest / len(cuts), largest / len(cuts))
        return jnp.repeat(jnp.exp(steps), dims[dim] // parts).reshape((-1,) + (1,) * (len(dims) - dim - 1))

    gain = one(*cuts[0])
    for cut in cuts[1:]:
        gain = gain * one(*cut)
    return gain


def normal_values(own_key, dims, spread, limit, shards=(), kind=jnp.bfloat16):
    factor_of = steps_of(own_key, dims, shards, -0.22, 0.18) if shards else 1.0
    entries = jax.random.normal(own_key, dims, jnp.float32) * spread * factor_of
    return jnp.minimum(jnp.maximum(entries, -limit), limit).astype(kind)


def setup_inputs(seed: int = 0) -> dict:
    keys = jax.random.split(jax.random.key(seed), 7)
    forcing = normal_values(keys[0], (L, NP, RC, DOF), 0.25, 1.5, ((0, 4), (1, 8)))
    iterate = normal_values(keys[1], (L, NP, RC, DOF), 0.25, 1.5, ((0, 4), (1, 8)))
    initial = normal_values(keys[2], (NP, RC, DOF), 0.25, 1.5, ((0, 8),))
    stiffness = normal_values(keys[3], (NP, DOF, DOF), DOF ** -0.5, 0.5, ((0, 8),))
    coupling = normal_values(keys[4], (NP, DOF, DOF), DOF ** -0.5, 0.5, ((0, 8),))
    pivots = normal_values(keys[5], (L, NP, 2, DOF, DOF), (DOF * 7 // 3) ** -0.5, 0.375, ((0, 4), (1, 8)))
    return dict(forcing=forcing, iterate=iterate, initial=initial, stiffness=stiffness, coupling=coupling, pivots=pivots)


PRECISE = lax.Precision.HIGHEST


def phase_table(row_ids, col_ids, total):
    turned = (row_ids[:, None] * col_ids[None, :]) % total
    angle = turned.astype(jnp.float32) * (2.0 * math.pi / total)
    return jnp.cos(angle), jnp.sin(angle)


def complex_product(left_real, left_imag, right_real, right_imag):
    form = "kcd,kde->kce"
    real_part = jnp.einsum(form, left_real, right_real, precision=PRECISE) - jnp.einsum(form, left_imag, right_imag, precision=PRECISE)
    imag_part = jnp.einsum(form, left_real, right_imag, precision=PRECISE) + jnp.einsum(form, left_imag, right_real, precision=PRECISE)
    return real_part, imag_part


def sweep_forward(spec_real, spec_imag, pivots, bonds, carry_real, carry_imag):
    count = spec_real.shape[1]

    def advance(plane_at, state):
        out_real, out_imag, into_real, into_imag = state
        pivot_now = lax.dynamic_index_in_dim(pivots, plane_at, 1, keepdims=False).astype(jnp.float32)
        bond = lax.dynamic_index_in_dim(bonds, plane_at, 0, keepdims=False)
        given_real = lax.dynamic_index_in_dim(spec_real, plane_at, 1, keepdims=False) - into_real
        given_imag = lax.dynamic_index_in_dim(spec_imag, plane_at, 1, keepdims=False) - into_imag
        pivot_real, pivot_imag = complex_product(given_real, given_imag, pivot_now[:, 0], pivot_now[:, 1])
        next_real = jnp.einsum("kcd,de->kce", pivot_real, bond, precision=PRECISE)
        next_imag = jnp.einsum("kcd,de->kce", pivot_imag, bond, precision=PRECISE)
        out_real = lax.dynamic_update_index_in_dim(out_real, pivot_real, plane_at, 1)
        out_imag = lax.dynamic_update_index_in_dim(out_imag, pivot_imag, plane_at, 1)
        return out_real, out_imag, next_real, next_imag

    start = (jnp.zeros_like(spec_real), jnp.zeros_like(spec_imag), carry_real, carry_imag)
    return lax.fori_loop(0, count, advance, start)


def sweep_backward(piv_real, piv_imag, pivots, bonds, carry_real, carry_imag):
    count = piv_real.shape[1]

    def retreat(step_at, state):
        out_real, out_imag, above_real, above_imag = state
        plane_at = count - 1 - step_at
        pivot_now = lax.dynamic_index_in_dim(pivots, plane_at, 1, keepdims=False).astype(jnp.float32)
        bond = lax.dynamic_index_in_dim(bonds, plane_at, 0, keepdims=False)
        bond_real = jnp.einsum("kce,de->kcd", above_real, bond, precision=PRECISE)
        bond_imag = jnp.einsum("kce,de->kcd", above_imag, bond, precision=PRECISE)
        mixed_real, mixed_imag = complex_product(bond_real, bond_imag, pivot_now[:, 0], pivot_now[:, 1])
        solved_real = lax.dynamic_index_in_dim(piv_real, plane_at, 1, keepdims=False) - mixed_real
        solved_imag = lax.dynamic_index_in_dim(piv_imag, plane_at, 1, keepdims=False) - mixed_imag
        out_real = lax.dynamic_update_index_in_dim(out_real, solved_real, plane_at, 1)
        out_imag = lax.dynamic_update_index_in_dim(out_imag, solved_imag, plane_at, 1)
        return out_real, out_imag, solved_real, solved_imag

    start = (jnp.zeros_like(piv_real), jnp.zeros_like(piv_imag), carry_real, carry_imag)
    return lax.fori_loop(0, count, retreat, start)


def reference(forcing, iterate, initial, stiffness, coupling, pivots):
    steps_all = iterate.shape[0]
    it_wide = iterate.astype(jnp.float32)
    prior_state = jnp.concatenate([initial[None], iterate[:-1]], 0)
    bonds = coupling.astype(jnp.float32)
    own_term = jnp.einsum("njcd,jde->njce", it_wide, stiffness.astype(jnp.float32))
    below = jnp.einsum("njcd,jde->njce", it_wide[:, :-1], bonds[:-1])
    above = jnp.einsum("njce,jde->njcd", it_wide[:, 1:], bonds[:-1])
    empty_plane = jnp.zeros_like(it_wide[:, :1])
    below = jnp.concatenate([empty_plane, below], 1)
    above = jnp.concatenate([above, empty_plane], 1)
    resid = forcing.astype(jnp.float32) - it_wide + prior_state.astype(jnp.float32) - (own_term + below + above)
    step_ids = jnp.arange(steps_all, dtype=jnp.int32)
    gamma = jnp.float32(0.5) ** (step_ids.astype(jnp.float32) / steps_all)
    scaled = resid * gamma[:, None, None, None]
    cosine, sine_table = phase_table(step_ids, step_ids, steps_all)
    spec_real = jnp.tensordot(cosine, scaled, axes=1, precision=PRECISE)
    spec_imag = -jnp.tensordot(sine_table, scaled, axes=1, precision=PRECISE)
    zero_vec = jnp.zeros_like(spec_real[:, 0])
    swept = sweep_forward(spec_real, spec_imag, pivots, bonds, zero_vec, zero_vec)
    solved = sweep_backward(swept[0], swept[1], pivots, bonds, zero_vec, zero_vec)
    correction = (jnp.tensordot(cosine, solved[0], axes=1, precision=PRECISE) - jnp.tensordot(sine_table, solved[1], axes=1, precision=PRECISE)) * (1.0 / steps_all)
    return it_wide + correction / gamma[:, None, None, None]
```

```python
import functools
import math

import jax
import jax.numpy as jnp
import numpy as np
from jax import lax
from jax.experimental import pallas as pl
from jax.experimental.pallas import tpu as pltpu
from jax.sharding import PartitionSpec as P

MESH = pl.DeviceIdType.MESH
F32 = jnp.float32
BF16 = jnp.bfloat16
GROUP = 4
PER = 2
LEAD = 2


def split(value):
    high = value.astype(BF16)
    low = (value - high.astype(F32)).astype(BF16)
    return high, low


def dot(a, b):
    return jnp.dot(a, b, preferred_element_type=F32)


def tables(total, blocks):
    ids = np.arange(total)
    theta = 2.0 * math.pi / total * ((ids[:, None] * ids[None, :]) % total)
    gamma = 0.5 ** (ids / total)
    here = total // blocks

    def three(table):
        high = table.astype(np.float32).astype(jnp.bfloat16)
        low = (table - high.astype(np.float64)).astype(np.float32).astype(jnp.bfloat16)
        return np.concatenate([high, high, low], -1)

    forward = np.stack([np.cos(theta) * gamma, -np.sin(theta) * gamma], 1)
    forward = three(forward.reshape(blocks, 2 * here, total))
    back = 1.0 / (total * gamma[:, None])
    inverse = np.stack([np.cos(theta) * back, -np.sin(theta) * back], 2)
    inverse = three(inverse.reshape(total, blocks, 2 * here).transpose(1, 0, 2))
    return forward, inverse


def kernel(
    n_tm, n_sp, group, per, cases, forcing_hbm, iterate_hbm, initial_hbm, stiff_hbm, coup_hbm,
    pivots_hbm, tf_hbm, ti_hbm, out,
    forcing, iterate, initial, stiff, bonds, pivots, tf, ti,
    it_below, it_above, prior0, gath, turned, spec, spec_out, pv, q_in, q_out, x_in, solved, fin,
    contrib, rs1, rs2,
    ld, nb_send, nb_recv, c_send, c_recv, p_send, p_recv, ag_send, ag_recv, s_send, s_recv,
    f_send, f_recv, b_send, b_recv, e_send, e_recv, r1_send, r1_recv, r2_send, r2_recv,
):
    tm, sp = lax.axis_index("tm"), lax.axis_index("span")
    rows, dof = iterate.shape
    steps = rows // cases
    total = steps * n_tm
    share = steps // group
    chunks = share // per
    state = 2 * cases
    size = per * state
    own_rows = share * state
    y = sp % 2
    m, g = sp % group, sp // group
    base = g * group
    n_g = n_sp // group
    n_x = n_tm // 2
    core, x = tm % 2, tm // 2
    sib = 2 * x + 1 - core
    last = n_sp - 1
    mates = [m + 1 - 2 * (m % 2)] + ([(m + 2) % 4, 3 - m] if group == 4 else [])
    has_next, has_prior = g < n_g - 1, g > 0
    pair_below, pair_above = sp > 1, sp < last - 1

    def copy(src, dst, send, recv, **where):
        return pltpu.make_async_remote_copy(
            src_ref=src, dst_ref=dst, send_sem=send, recv_sem=recv, device_id=where, device_id_type=MESH
        )

    loads = [
        pltpu.make_async_copy(src, dst, ld.at[i])
        for i, (src, dst) in enumerate(
            (
                (iterate_hbm, iterate),
                (stiff_hbm, stiff),
                (forcing_hbm, forcing),
                (initial_hbm, initial),
                (coup_hbm, bonds.at[m + 1]),
                (tf_hbm.at[tm], tf),
                (ti_hbm.at[tm], ti),
                (pivots_hbm.at[pl.ds(m * share, share)], pivots.at[m]),
            )
        )
    ]
    for load in loads:
        load.start()

    def block(b):
        return pl.ds(pl.multiple_of(b * rows, rows), rows)

    barrier = pltpu.get_barrier_semaphore()
    for i in range(1, n_tm):
        pl.semaphore_signal(barrier, inc=1, device_id={"tm": (tm + i) % n_tm}, device_id_type=MESH)
    greeted = n_tm - 1
    for d in range(1, group + 1):
        near = d in (1, 2, group)
        up_ok = sp + d <= last if near else m + d < group
        down_ok = sp >= d if near else m >= d
        for ok, there in ((up_ok, sp + d), (down_ok, sp - d)):
            @pl.when(ok)
            def _():
                pl.semaphore_signal(barrier, inc=1, device_id={"span": there}, device_id_type=MESH)

            greeted = greeted + ok.astype(jnp.int32)
    pl.semaphore_wait(barrier, greeted)

    to_up = copy(iterate_hbm, it_below, nb_send.at[0], nb_recv.at[0], span=sp + 1)
    to_down = copy(iterate_hbm, it_above, nb_send.at[1], nb_recv.at[1], span=sp - 1)
    on_up = copy(it_above, it_below, nb_send.at[2], nb_recv.at[2], span=sp + 2)
    on_down = copy(it_below, it_above, nb_send.at[3], nb_recv.at[3], span=sp - 2)
    to_next = copy(
        iterate_hbm.at[pl.ds(rows - cases, cases)], prior0, nb_send.at[4], nb_recv.at[4], tm=tm + 1
    )
    c_next = copy(coup_hbm, bonds.at[0], c_send.at[group], c_recv.at[0], span=sp + 1)
    gives_c = (m == group - 1) & has_next

    def c_copy(i):
        return copy(
            coup_hbm, bonds.at[m + 1], c_send.at[i], c_recv.at[m + 1], span=base + mates[i]
        )

    def c_wait(slot):
        copy(coup_hbm, bonds.at[slot], c_send.at[0], c_recv.at[slot], span=sp).wait_recv()

    def p_copy(i, f):
        return copy(
            pivots_hbm.at[mates[i] * share + f], pivots.at[m, f], p_send.at[i, f], p_recv.at[m, f],
            span=base + mates[i],
        )

    def p_wait(i, f):
        copy(
            pivots_hbm.at[f], pivots.at[mates[i], f], p_send.at[i, f], p_recv.at[mates[i], f],
            span=sp,
        ).wait_recv()

    def p_start(*pairs):
        for i, f in pairs:
            if i < group - 1:
                p_copy(i, f).start()

    part = [range(k * share // 4, (k + 1) * share // 4) for k in range(4)]
    late = [(i, f) for f in range(share // 2, share) for i in (1, 2)]

    @pl.when(tm < n_tm - 1)
    def _():
        to_next.start()

    @pl.when(y == 0)
    def _():
        to_up.start()

    @pl.when(y == 1)
    def _():
        to_down.start()

    for i in range(group - 1):
        c_copy(i).start()

    @pl.when(gives_c)
    def _():
        c_next.start()

    p_start(*[(i, f) for f in part[0] for i in (1, 0)])

    mine = block(tm)
    for load in loads[:5]:
        load.wait()
    it_wide = iterate[...].astype(F32)
    own = forcing[...].astype(F32) - it_wide - dot(iterate[...], stiff[...])
    own = own + jnp.concatenate([jnp.zeros((cases, dof), F32), it_wide[: rows - cases]], 0)
    gath[mine] = own
    first = pl.ds(pl.multiple_of(tm * rows, rows), cases)

    @pl.when(tm == 0)
    def _():
        gath[first] = gath[first] + initial[...].astype(F32)

    @pl.when(tm > 0)
    def _():
        to_next.wait_recv()
        gath[first] = gath[first] + prior0[...].astype(F32)

    @pl.when(y == 0)
    def _():
        to_down.wait_recv()

        @pl.when(pair_above)
        def _():
            on_up.start()

    @pl.when(y == 1)
    def _():
        to_up.wait_recv()

        @pl.when(pair_below)
        def _():
            on_down.start()

    p_start(*[(0, f) for f in part[1]], *[(2, f) for f in part[0]])

    def from_above():
        gath[mine] = gath[mine] - lax.dot_general(
            it_above[...], bonds[m + 1], (((1,), (1,)), ((), ())), preferred_element_type=F32
        )

    def from_below():
        c_wait(m)
        gath[mine] = gath[mine] - dot(it_below[...], bonds[m])

    @pl.when(y == 0)
    def _():
        from_above()

        @pl.when(pair_below)
        def _():
            on_up.wait_recv()
            from_below()

    @pl.when(y == 1)
    def _():
        from_below()

        @pl.when(pair_above)
        def _():
            on_down.wait_recv()
            from_above()

    def send_block(b, slot, peer):
        at = block(b)
        return copy(gath.at[at], gath.at[at], ag_send.at[slot], ag_recv.at[b], tm=peer)

    for i in range(1, n_x):
        send_block(tm, i, 2 * ((x + i) % n_x) + core).start()
    send_block(tm, 0, sib).start()

    p_start(*[(i, f) for f in part[1] for i in (1, 2)], *[(0, f) for f in part[2]])

    for i in range(1, group - 1):
        c_wait((m + i) % group + 1)

    @pl.when(m == 0)
    def _():
        c_wait(group)

    for p in range(group):
        turned[p] = bonds[p + 1].astype(F32).T.astype(BF16)

    @pl.when(g == 0)
    def _():
        q_in[...] = jnp.zeros_like(q_in)

    for load in loads[5:]:
        load.wait()
    for i in range(1, n_x):
        b = 2 * ((x + n_x - i) % n_x) + core
        send_block(b, 0, sib).wait_recv()
        send_block(b, n_x + i, sib).start()
    for i in range(n_x):
        send_block(2 * ((x + n_x - i) % n_x) + 1 - core, 0, sib).wait_recv()

    def at_chunk(c):
        return pl.ds(pl.multiple_of(c * size, size), size)

    def s_copy(i, c):
        at = at_chunk(c)
        return copy(
            spec_out.at[mates[i], at], spec.at[m, at], s_send.at[i, c], s_recv.at[m, c],
            span=base + mates[i],
        )

    def s_wait(i, c):
        at = at_chunk(c)
        copy(
            spec_out.at[mates[i], at], spec.at[mates[i], at], s_send.at[i, c],
            s_recv.at[mates[i], c], span=sp,
        ).wait_recv()

    for case in range(0, cases, 2):
        value = jnp.concatenate(
            [gath[pl.ds(case + i, total, stride=cases), :] for i in range(2)], 1
        )
        high, low = split(value)
        result = dot(tf[...], jnp.concatenate([high, low, high], 0))
        for r in range(group):
            for i in range(2):
                spec_out[r, pl.ds(case + i, 2 * share, stride=cases), :] = result[
                    r * 2 * share : (r + 1) * 2 * share, i * dof : (i + 1) * dof
                ]
    for c in range(chunks):
        for i in range(group - 1):
            s_copy(i, c).start()
    p_start(*late[:2], *[(0, f) for f in part[3]])
    spec[m] = spec_out[m]

    def f_copy(c):
        at = at_chunk(c)
        return copy(q_out.at[at], q_in.at[at], f_send.at[c], f_recv.at[c], span=sp + group)

    def b_copy(c):
        at = at_chunk(c)
        return copy(solved.at[0, at], x_in.at[at], b_send.at[c], b_recv.at[c], span=sp - group)

    def at_fin(q, c):
        return pl.ds(pl.multiple_of(q * own_rows + c * size, size), size)

    def e_copy(i, c):
        return copy(
            solved.at[mates[i], at_chunk(c)], fin.at[at_fin(m, c)], e_send.at[i, c],
            e_recv.at[m, c], span=base + mates[i],
        )

    def e_wait(i, c):
        copy(
            solved.at[mates[i], at_chunk(c)], fin.at[at_fin(mates[i], c)], e_send.at[i, c],
            e_recv.at[mates[i], c], span=sp,
        ).wait_recv()

    def times_pivots(value, p, c):
        high, low = split(value)
        parts = []
        for f in range(per):
            at = slice(f * state, (f + 1) * state)
            factor = jnp.concatenate([pivots[p, c * per + f, 0], pivots[p, c * per + f, 1]], 1)
            both = dot(jnp.concatenate([high[at], low[at]], 0), factor)
            both = both[:state] + both[state:]
            parts.append(both[:cases, :dof] - both[cases:, dof:])
            parts.append(both[:cases, dof:] + both[cases:, :dof])
        return jnp.concatenate(parts, 0)

    def times_bond(value, bond):
        both = dot(jnp.concatenate(split(value), 0), bond)
        return both[:size] + both[size:]

    def finish(c, at, top, lower):
        solved[group - 1, at] = top
        for p in range(group - 2, -1, -1):
            top = lower(p) - times_pivots(times_bond(top, turned[p]), p, c)
            solved[p, at] = top

        @pl.when(has_prior)
        def _():
            b_copy(c).start()

        for i in range(group - 1):
            e_copy(i, c).start()
        fin[at_fin(m, c)] = solved[m, at]

    def up(c):
        at = at_chunk(c)
        for i in range(group - 1):
            for f in range(per):
                p_wait(i, c * per + f)
            s_wait(i, c)

        @pl.when(has_prior)
        def _():
            f_copy(c).wait_recv()

        done = []
        carried = q_in[at]
        for p in range(group):
            done.append(times_pivots(spec[p, at] - carried, p, c))
            if p < group - 1:
                carried = times_bond(done[p], bonds[p + 1])

        @pl.when(has_next)
        def _():
            q_out[at] = times_bond(done[-1], bonds[group])
            f_copy(c).start()
            for p in range(group):
                pv[p, at] = done[p]

        @pl.when(g == n_g - 1)
        def _():
            finish(c, at, done[-1], lambda p: done[p])

    def down(c):
        at = at_chunk(c)
        b_copy(c).wait_recv()
        top = pv[group - 1, at] - times_pivots(
            times_bond(x_in[at], turned[group - 1]), group - 1, c
        )
        finish(c, at, top, lambda p: pv[p, at])

    lag = jnp.minimum(chunks, LEAD * (n_g - 1 - g))

    def p_more(t):
        for at, pairs in ((0, late[2:5]), (min(1, chunks - 1), late[5:])):
            @pl.when(t == at)
            def _():
                p_start(*pairs)

    def turn(t, carry):
        @pl.when(has_prior)
        def _():
            p_more(t)

        @pl.when(t < chunks)
        def _():
            up(t)

        @pl.when(g == 0)
        def _():
            p_more(t)

        @pl.when(has_next & (t >= lag) & (t < lag + chunks))
        def _():
            down(t - lag)

        return carry

    lax.fori_loop(0, 2 * chunks, turn, 0)
    for c in range(chunks):
        for i in range(group - 1):
            e_wait(i, c)

    for case in range(0, cases, 2):
        value = jnp.concatenate(
            [fin[pl.ds(case + i, 2 * steps, stride=cases), :] for i in range(2)], 1
        )
        high, low = split(value)
        result = dot(ti[...], jnp.concatenate([high, low, high], 0))
        for i in range(2):
            contrib[pl.ds(case + i, total, stride=cases), :] = result[:, i * dof : (i + 1) * dof]

    def r1_copy(i):
        there = (x + i) % n_x
        return copy(
            contrib.at[block(2 * there + 1 - core)], rs1.at[i], r1_send.at[i], r1_recv.at[i], tm=sib
        )

    def r2_copy(i):
        there = (x + i) % n_x
        return copy(
            contrib.at[block(2 * there + core)], rs2.at[i], r2_send.at[i], r2_recv.at[i],
            tm=2 * there + core,
        )

    order = list(range(1, n_x)) + [0]
    for i in order:
        r1_copy(i).start()
    for i in order:
        r1_copy(i).wait_recv()
        at = block(2 * ((x + i) % n_x) + core)
        contrib[at] = contrib[at] + rs1[i]
        if i:
            r2_copy(i).start()
    result = contrib[mine] + iterate[...].astype(F32)
    for i in range(1, n_x):
        r2_copy(i).wait_recv()
        result = result + rs2[i]
    out[...] = result

    @pl.when(tm < n_tm - 1)
    def _():
        to_next.wait_send()

    @pl.when(y == 0)
    def _():
        to_up.wait_send()

        @pl.when(pair_above)
        def _():
            on_up.wait_send()

    @pl.when(y == 1)
    def _():
        to_down.wait_send()

        @pl.when(pair_below)
        def _():
            on_down.wait_send()

    @pl.when(gives_c)
    def _():
        c_next.wait_send()

    for slot in range(2 * n_x):
        if slot != n_x:
            send_block(tm, slot, sib).wait_send()

    for i in range(group - 1):
        c_copy(i).wait_send()
        for f in range(share):
            p_copy(i, f).wait_send()
        for c in range(chunks):
            s_copy(i, c).wait_send()
            e_copy(i, c).wait_send()

    @pl.when(has_next)
    def _():
        for c in range(chunks):
            f_copy(c).wait_send()

    @pl.when(has_prior)
    def _():
        for c in range(chunks):
            b_copy(c).wait_send()

    for i in range(n_x):
        r1_copy(i).wait_send()
    for i in range(1, n_x):
        r2_copy(i).wait_send()


def on_device(n_tm, n_sp, forcing, iterate, initial, stiffness, coupling, pivots):
    steps, planes, cases, dof = forcing.shape
    group = GROUP if n_sp % GROUP == 0 else 2
    assert planes == 1 and n_tm % 2 == 0 and n_sp % 2 == 0 and steps % group == 0
    rows, total, n_x, share = steps * cases, steps * n_tm, n_tm // 2, steps // group
    per = math.gcd(share, PER)
    chunks = share // per
    forward, inverse = tables(total, n_tm)
    own = share * 2 * cases
    state = pltpu.VMEM((own, dof), F32)
    planes_of = pltpu.VMEM((group, own, dof), F32)
    dma = pltpu.SemaphoreType.DMA
    each = [dma((group - 1, chunks)), dma((group, chunks))]
    result = pl.pallas_call(
        functools.partial(kernel, n_tm, n_sp, group, per, cases),
        out_shape=jax.ShapeDtypeStruct((rows, dof), F32),
        in_specs=[pl.BlockSpec(memory_space=pltpu.HBM)] * 8,
        out_specs=pl.BlockSpec(memory_space=pltpu.VMEM),
        scratch_shapes=[
            pltpu.VMEM((rows, dof), BF16),
            pltpu.VMEM((rows, dof), BF16),
            pltpu.VMEM((cases, dof), BF16),
            pltpu.VMEM((dof, dof), BF16),
            pltpu.VMEM((group + 1, dof, dof), BF16),
            pltpu.VMEM((group, share, 2, dof, dof), BF16),
            pltpu.VMEM(forward.shape[1:], BF16),
            pltpu.VMEM(inverse.shape[1:], BF16),
            pltpu.VMEM((rows, dof), BF16),
            pltpu.VMEM((rows, dof), BF16),
            pltpu.VMEM((cases, dof), BF16),
            pltpu.VMEM((total * cases, dof), F32),
            pltpu.VMEM((group, dof, dof), BF16),
            planes_of, planes_of, planes_of, state, state, state, planes_of,
            pltpu.VMEM((group * own, dof), F32),
            pltpu.VMEM((total * cases, dof), F32),
            pltpu.VMEM((n_x, rows, dof), F32),
            pltpu.VMEM((n_x, rows, dof), F32),
            dma((8,)), dma((5,)), dma((5,)), dma((group + 1,)), dma((group + 1,)),
            dma((group - 1, share)), dma((group, share)), dma((2 * n_x,)), dma((n_tm,)), *each,
            dma((chunks,)), dma((chunks,)), dma((chunks,)), dma((chunks,)), *each,
            dma((n_x,)), dma((n_x,)), dma((n_x,)), dma((n_x,)),
        ],
        compiler_params=pltpu.CompilerParams(
            collective_id=0, has_side_effects=True, vmem_limit_bytes=16 * 2**20
        ),
    )(
        *[
            pltpu.with_memory_space_constraint(value, pltpu.HBM)
            for value in (
                forcing.reshape(rows, dof),
                iterate.reshape(rows, dof),
                initial.reshape(cases, dof),
                stiffness.reshape(dof, dof),
                coupling.reshape(dof, dof),
                pivots.reshape(steps, 2, dof, dof),
                jnp.asarray(forward),
                jnp.asarray(inverse),
            )
        ]
    )
    return result.reshape(steps, 1, cases, dof)


def solution(mesh):
    return jax.shard_map(
        functools.partial(on_device, mesh.shape["tm"], mesh.shape["span"]),
        mesh=mesh,
        in_specs=(
            P("tm", "span", None, None),
            P("tm", "span", None, None),
            P("span", None, None),
            P("span", None, None),
            P("span", None, None),
            P("tm", "span", None, None, None),
        ),
        out_specs=P("tm", "span", None, None),
        check_vma=False,
    )
```

```python
import functools
import math

import jax
import jax.numpy as jnp
import numpy as np
from jax import lax
from jax.experimental import pallas as pl
from jax.experimental.pallas import tpu as pltpu
from jax.sharding import PartitionSpec as P

MESH = pl.DeviceIdType.MESH
F32 = jnp.float32
BF16 = jnp.bfloat16
GROUP = 4
PER = 2
LEAD = 2
PIECES = 4
CODE = 14.0
TOP = 120.0
MARK = 16


def split(value):
    high = value.astype(BF16)
    low = (value - high.astype(F32)).astype(BF16)
    return high, low


def dot(a, b):
    return jnp.dot(a, b, preferred_element_type=F32)


def encode(value, out):
    rows, lanes = value.shape
    size = jnp.maximum(jnp.abs(value), 1e-37)
    e = jnp.max(jnp.max(size, 0, keepdims=True), 1, keepdims=True)
    e = jnp.ceil(jnp.log2(jnp.maximum(e, 1e-29)))
    power = jnp.exp2(CODE * (jnp.log2(size) - e) + TOP)
    out[:MARK] = jnp.broadcast_to(e, (MARK, lanes)).astype(BF16)
    out[MARK:] = jnp.where(value < 0, -power, power).astype(BF16)


def decode(mark, power):
    power, e = power.astype(F32), mark.astype(F32)[:1]
    size = jnp.exp2((jnp.log2(jnp.maximum(jnp.abs(power), 1e-37)) - TOP) * (1.0 / CODE) + e)
    return jnp.where(power == 0, 0.0, jnp.where(power < 0, -size, size))


def tables(total, blocks):
    ids = np.arange(total)
    theta = 2.0 * math.pi / total * ((ids[:, None] * ids[None, :]) % total)
    gamma = 0.5 ** (ids / total)
    here = total // blocks

    def three(table):
        high = table.astype(np.float32).astype(jnp.bfloat16)
        low = (table - high.astype(np.float64)).astype(np.float32).astype(jnp.bfloat16)
        return np.concatenate([high, high, low], -1)

    forward = np.stack([np.cos(theta) * gamma, -np.sin(theta) * gamma], 1)
    forward = three(forward.reshape(blocks, 2 * here, total))
    back = 1.0 / (total * gamma[:, None])
    inverse = np.stack([np.cos(theta) * back, -np.sin(theta) * back], 2)
    inverse = three(inverse.reshape(total, blocks, 2 * here).transpose(1, 0, 2))
    return forward, inverse


def kernel(
    n_tm, n_sp, group, per, cases, forcing_hbm, iterate_hbm, initial_hbm, stiff_hbm, coup_hbm,
    pivots_hbm, tf_hbm, ti_hbm, out,
    forcing, iterate, initial, stiff, bonds, pivots, tf, ti,
    it_below, it_above, prior0, gath, turned, spec, spec_out, code_out, code_in, pv, q_in, q_out, x_in, solved, fin,
    contrib, rs1, sums_out, sums_in,
    ld, nb_send, nb_recv, c_send, c_recv, p_send, p_recv, ag_send, ag_recv, s_send, s_recv,
    f_send, f_recv, b_send, b_recv, e_send, e_recv, r1_send, r1_recv, r2_send, r2_recv, o_sem,
):
    tm, sp = lax.axis_index("tm"), lax.axis_index("span")
    rows, dof = iterate.shape
    steps = rows // cases
    total = steps * n_tm
    share = steps // group
    chunks = share // per
    state = 2 * cases
    size = per * state
    own_rows = share * state
    y = sp % 2
    m, g = sp % group, sp // group
    base = g * group
    n_g = n_sp // group
    n_x = n_tm // 2
    core, x = tm % 2, tm // 2
    sib = 2 * x + 1 - core
    last = n_sp - 1
    mates = [m + 1 - 2 * (m % 2)] + ([(m + 2) % 4, 3 - m] if group == 4 else [])
    has_next, has_prior = g < n_g - 1, g > 0
    pair_below, pair_above = sp > 1, sp < last - 1

    def copy(src, dst, send, recv, **where):
        return pltpu.make_async_remote_copy(
            src_ref=src, dst_ref=dst, send_sem=send, recv_sem=recv, device_id=where, device_id_type=MESH
        )

    loads = [
        pltpu.make_async_copy(src, dst, ld.at[i])
        for i, (src, dst) in enumerate(
            (
                (iterate_hbm, iterate),
                (stiff_hbm, stiff),
                (forcing_hbm, forcing),
                (initial_hbm, initial),
                (coup_hbm, bonds.at[m + 1]),
                (tf_hbm.at[tm], tf),
                (ti_hbm.at[tm], ti),
                (pivots_hbm.at[pl.ds(m * share, share)], pivots.at[m]),
            )
        )
    ]
    for load in loads:
        load.start()

    def block(b):
        return pl.ds(pl.multiple_of(b * rows, rows), rows)

    barrier = pltpu.get_barrier_semaphore()
    for i in range(1, n_tm):
        pl.semaphore_signal(barrier, inc=1, device_id={"tm": (tm + i) % n_tm}, device_id_type=MESH)
    greeted = n_tm - 1
    for d in range(1, group + 1):
        near = d in (1, 2, group)
        up_ok = sp + d <= last if near else m + d < group
        down_ok = sp >= d if near else m >= d
        for ok, there in ((up_ok, sp + d), (down_ok, sp - d)):
            @pl.when(ok)
            def _():
                pl.semaphore_signal(barrier, inc=1, device_id={"span": there}, device_id_type=MESH)

            greeted = greeted + ok.astype(jnp.int32)
    pl.semaphore_wait(barrier, greeted)

    to_up = copy(iterate_hbm, it_below, nb_send.at[0], nb_recv.at[0], span=sp + 1)
    to_down = copy(iterate_hbm, it_above, nb_send.at[1], nb_recv.at[1], span=sp - 1)
    on_up = copy(it_above, it_below, nb_send.at[2], nb_recv.at[2], span=sp + 2)
    on_down = copy(it_below, it_above, nb_send.at[3], nb_recv.at[3], span=sp - 2)
    to_next = copy(
        iterate_hbm.at[pl.ds(rows - cases, cases)], prior0, nb_send.at[4], nb_recv.at[4], tm=tm + 1
    )
    c_next = copy(coup_hbm, bonds.at[0], c_send.at[group], c_recv.at[0], span=sp + 1)
    gives_c = (m == group - 1) & has_next

    def c_copy(i):
        return copy(
            coup_hbm, bonds.at[m + 1], c_send.at[i], c_recv.at[m + 1], span=base + mates[i]
        )

    def c_wait(slot):
        copy(coup_hbm, bonds.at[slot], c_send.at[0], c_recv.at[slot], span=sp).wait_recv()

    def p_copy(i, f):
        return copy(
            pivots_hbm.at[mates[i] * share + f], pivots.at[m, f], p_send.at[i, f], p_recv.at[m, f],
            span=base + mates[i],
        )

    def p_wait(i, f):
        copy(
            pivots_hbm.at[f], pivots.at[mates[i], f], p_send.at[i, f], p_recv.at[mates[i], f],
            span=sp,
        ).wait_recv()

    def p_start(*pairs):
        for i, f in pairs:
            if i < group - 1:
                p_copy(i, f).start()

    part = [range(k * share // 4, (k + 1) * share // 4) for k in range(4)]
    late = [(i, f) for f in range(share // 2, share) for i in (1, 2)]

    @pl.when(tm < n_tm - 1)
    def _():
        to_next.start()

    @pl.when(y == 0)
    def _():
        to_up.start()

    @pl.when(y == 1)
    def _():
        to_down.start()

    for i in range(group - 1):
        c_copy(i).start()

    @pl.when(gives_c)
    def _():
        c_next.start()

    p_start(*[(i, f) for f in part[0] for i in (1, 0)])

    mine = block(tm)
    for load in loads[:5]:
        load.wait()
    it_wide = iterate[...].astype(F32)
    own = forcing[...].astype(F32) - it_wide - dot(iterate[...], stiff[...])
    own = own + jnp.concatenate([jnp.zeros((cases, dof), F32), it_wide[: rows - cases]], 0)
    gath[mine] = own
    first = pl.ds(pl.multiple_of(tm * rows, rows), cases)

    @pl.when(tm == 0)
    def _():
        gath[first] = gath[first] + initial[...].astype(F32)

    @pl.when(tm > 0)
    def _():
        to_next.wait_recv()
        gath[first] = gath[first] + prior0[...].astype(F32)

    @pl.when(y == 0)
    def _():
        to_down.wait_recv()

        @pl.when(pair_above)
        def _():
            on_up.start()

    @pl.when(y == 1)
    def _():
        to_up.wait_recv()

        @pl.when(pair_below)
        def _():
            on_down.start()

    p_start(*[(0, f) for f in part[1]], *[(2, f) for f in part[0]])

    def from_above():
        gath[mine] = gath[mine] - lax.dot_general(
            it_above[...], bonds[m + 1], (((1,), (1,)), ((), ())), preferred_element_type=F32
        )

    def from_below():
        c_wait(m)
        gath[mine] = gath[mine] - dot(it_below[...], bonds[m])

    @pl.when(y == 0)
    def _():
        from_above()

        @pl.when(pair_below)
        def _():
            on_up.wait_recv()
            from_below()

    @pl.when(y == 1)
    def _():
        from_below()

        @pl.when(pair_above)
        def _():
            on_down.wait_recv()
            from_above()

    def send_block(b, slot, peer):
        at = block(b)
        return copy(gath.at[at], gath.at[at], ag_send.at[slot], ag_recv.at[b], tm=peer)

    for i in range(1, n_x):
        send_block(tm, i, 2 * ((x + i) % n_x) + core).start()
    send_block(tm, 0, sib).start()

    p_start(*[(i, f) for f in part[1] for i in (1, 2)], *[(0, f) for f in part[2]])

    for i in range(1, group - 1):
        c_wait((m + i) % group + 1)

    @pl.when(m == 0)
    def _():
        c_wait(group)

    for p in range(group):
        turned[p] = bonds[p + 1].astype(F32).T.astype(BF16)

    @pl.when(g == 0)
    def _():
        q_in[...] = jnp.zeros_like(q_in)

    for load in loads[5:]:
        load.wait()
    for i in range(1, n_x):
        b = 2 * ((x + n_x - i) % n_x) + core
        send_block(b, 0, sib).wait_recv()
        send_block(b, n_x + i, sib).start()
    for i in range(n_x):
        send_block(2 * ((x + n_x - i) % n_x) + 1 - core, 0, sib).wait_recv()

    def at_chunk(c):
        return pl.ds(pl.multiple_of(c * size, size), size)

    def s_copy(i, c):
        start, count = (0, MARK + size) if c == 0 else (MARK + c * size, size)
        at = pl.ds(start, count)
        return copy(
            code_out.at[i, at], code_in.at[m, at], s_send.at[i, c], s_recv.at[m, c],
            span=base + mates[i],
        )

    def s_wait(i, c):
        source = mates[i]

        @pl.when(c == 0)
        def _():
            copy(
                code_out.at[i, pl.ds(0, MARK + size)], code_in.at[source, pl.ds(0, MARK + size)],
                s_send.at[i, c], s_recv.at[source, c], span=sp,
            ).wait_recv()

        at = pl.ds(pl.multiple_of(MARK + c * size, MARK), size)

        @pl.when(c > 0)
        def _():
            copy(
                code_out.at[i, at], code_in.at[source, at], s_send.at[i, c],
                s_recv.at[source, c], span=sp,
            ).wait_recv()

        spec[source, at_chunk(c)] = decode(code_in[source, :MARK], code_in[source, at])

    for case in range(0, cases, 2):
        value = jnp.concatenate(
            [gath[pl.ds(case + i, total, stride=cases), :] for i in range(2)], 1
        )
        high, low = split(value)
        result = dot(tf[...], jnp.concatenate([high, low, high], 0))
        for r in range(group):
            for i in range(2):
                spec_out[r, pl.ds(case + i, 2 * share, stride=cases), :] = result[
                    r * 2 * share : (r + 1) * 2 * share, i * dof : (i + 1) * dof
                ]
    for i in range(group - 1):
        encode(spec_out[mates[i]], code_out.at[i])
    for c in range(chunks):
        for i in range(group - 1):
            s_copy(i, c).start()
    p_start(*late[:2], *[(0, f) for f in part[3]])
    spec[m] = spec_out[m]

    def f_copy(c):
        at = at_chunk(c)
        return copy(q_out.at[at], q_in.at[at], f_send.at[c], f_recv.at[c], span=sp + group)

    def b_copy(c):
        at = at_chunk(c)
        return copy(solved.at[0, at], x_in.at[at], b_send.at[c], b_recv.at[c], span=sp - group)

    def at_fin(q, c):
        return pl.ds(pl.multiple_of(q * own_rows + c * size, size), size)

    def e_copy(i, c):
        return copy(
            solved.at[mates[i], at_chunk(c)], fin.at[at_fin(m, c)], e_send.at[i, c],
            e_recv.at[m, c], span=base + mates[i],
        )

    def e_wait(i, c):
        copy(
            solved.at[mates[i], at_chunk(c)], fin.at[at_fin(mates[i], c)], e_send.at[i, c],
            e_recv.at[mates[i], c], span=sp,
        ).wait_recv()

    def times_pivots(value, p, c):
        high, low = split(value)
        parts = []
        for f in range(per):
            at = slice(f * state, (f + 1) * state)
            factor = jnp.concatenate([pivots[p, c * per + f, 0], pivots[p, c * per + f, 1]], 1)
            both = dot(jnp.concatenate([high[at], low[at]], 0), factor)
            both = both[:state] + both[state:]
            parts.append(both[:cases, :dof] - both[cases:, dof:])
            parts.append(both[:cases, dof:] + both[cases:, :dof])
        return jnp.concatenate(parts, 0)

    def times_bond(value, bond):
        both = dot(jnp.concatenate(split(value), 0), bond)
        return both[:size] + both[size:]

    def finish(c, at, top, lower):
        solved[group - 1, at] = top
        for p in range(group - 2, -1, -1):
            top = lower(p) - times_pivots(times_bond(top, turned[p]), p, c)
            solved[p, at] = top

        @pl.when(has_prior)
        def _():
            b_copy(c).start()

        for i in range(group - 1):
            e_copy(i, c).start()
        fin[at_fin(m, c)] = solved[m, at]

    def up(c):
        at = at_chunk(c)
        for i in range(group - 1):
            for f in range(per):
                p_wait(i, c * per + f)
            s_wait(i, c)

        @pl.when(has_prior)
        def _():
            f_copy(c).wait_recv()

        done = []
        carried = q_in[at]
        for p in range(group):
            done.append(times_pivots(spec[p, at] - carried, p, c))
            if p < group - 1:
                carried = times_bond(done[p], bonds[p + 1])

        @pl.when(has_next)
        def _():
            q_out[at] = times_bond(done[-1], bonds[group])
            f_copy(c).start()
            for p in range(group):
                pv[p, at] = done[p]

        @pl.when(g == n_g - 1)
        def _():
            finish(c, at, done[-1], lambda p: done[p])

    def down(c):
        at = at_chunk(c)
        b_copy(c).wait_recv()
        top = pv[group - 1, at] - times_pivots(
            times_bond(x_in[at], turned[group - 1]), group - 1, c
        )
        finish(c, at, top, lambda p: pv[p, at])

    lag = jnp.minimum(chunks, LEAD * (n_g - 1 - g))

    def p_more(t):
        for at, pairs in ((0, late[2:5]), (min(1, chunks - 1), late[5:])):
            @pl.when(t == at)
            def _():
                p_start(*pairs)

    def turn(t, carry):
        @pl.when(has_prior)
        def _():
            p_more(t)

        @pl.when(t < chunks)
        def _():
            up(t)

        @pl.when(g == 0)
        def _():
            p_more(t)

        @pl.when(has_next & (t >= lag) & (t < lag + chunks))
        def _():
            down(t - lag)

        return carry

    lax.fori_loop(0, 2 * chunks, turn, 0)
    for c in range(chunks):
        for i in range(group - 1):
            e_wait(i, c)

    for case in range(0, cases, 2):
        value = jnp.concatenate(
            [fin[pl.ds(case + i, 2 * steps, stride=cases), :] for i in range(2)], 1
        )
        high, low = split(value)
        result = dot(ti[...], jnp.concatenate([high, low, high], 0))
        for i in range(2):
            contrib[pl.ds(case + i, total, stride=cases), :] = result[:, i * dof : (i + 1) * dof]

    piece = rows // PIECES

    def at_piece(b, j):
        return pl.ds(pl.multiple_of(b * rows + j * piece, piece), piece)

    def r1_copy(i, j):
        there = (x + i) % n_x
        return copy(
            contrib.at[at_piece(2 * there + 1 - core, j)], rs1.at[i, pl.ds(j * piece, piece)],
            r1_send.at[i, j], r1_recv.at[i, j], tm=sib,
        )

    def r2_copy(i, j):
        return copy(
            sums_out.at[i, j], sums_in.at[i, j], r2_send.at[i, j], r2_recv.at[i, j],
            tm=2 * ((x + i) % n_x) + core,
        )

    for i in list(range(1, n_x)) + [0]:
        for j in range(PIECES):
            r1_copy(i, j).start()
    for i in range(1, n_x):
        for j in range(PIECES):
            r1_copy(i, j).wait_recv()
            at = at_piece(2 * ((x + i) % n_x) + core, j)
            encode(contrib[at] + rs1[i, pl.ds(j * piece, piece)], sums_out.at[i, j])
            r2_copy(i, j).start()
    @pl.when(tm < n_tm - 1)
    def _():
        to_next.wait_send()

    @pl.when(y == 0)
    def _():
        to_up.wait_send()

        @pl.when(pair_above)
        def _():
            on_up.wait_send()

    @pl.when(y == 1)
    def _():
        to_down.wait_send()

        @pl.when(pair_below)
        def _():
            on_down.wait_send()

    @pl.when(gives_c)
    def _():
        c_next.wait_send()

    for slot in range(2 * n_x):
        if slot != n_x:
            send_block(tm, slot, sib).wait_send()

    for i in range(group - 1):
        c_copy(i).wait_send()
        for f in range(share):
            p_copy(i, f).wait_send()
        for c in range(chunks):
            s_copy(i, c).wait_send()
            e_copy(i, c).wait_send()

    @pl.when(has_next)
    def _():
        for c in range(chunks):
            f_copy(c).wait_send()

    @pl.when(has_prior)
    def _():
        for c in range(chunks):
            b_copy(c).wait_send()

    for j in range(PIECES):
        r1_copy(0, j).wait_recv()
        own = iterate[pl.ds(j * piece, piece)].astype(F32) + rs1[0, pl.ds(j * piece, piece)]
        rs1[0, pl.ds(j * piece, piece)] = own + contrib[at_piece(tm, j)]
    for i in range(n_x):
        for j in range(PIECES):
            r1_copy(i, j).wait_send()

    def o_copy(j):
        at = pl.ds(j * piece, piece)
        return pltpu.make_async_copy(rs1.at[0, at], out.at[at], o_sem.at[j])

    for j in range(PIECES):
        result = rs1[0, pl.ds(j * piece, piece)]
        for i in range(1, n_x):
            r2_copy(i, j).wait_recv()
            result = result + decode(sums_in[i, j, :MARK], sums_in[i, j, MARK:])
        rs1[0, pl.ds(j * piece, piece)] = result
        o_copy(j).start()
    for j in range(PIECES):
        o_copy(j).wait()
        for i in range(1, n_x):
            r2_copy(i, j).wait_send()


def on_device(n_tm, n_sp, forcing, iterate, initial, stiffness, coupling, pivots):
    steps, planes, cases, dof = forcing.shape
    group = GROUP if n_sp % GROUP == 0 else 2
    assert planes == 1 and n_tm % 2 == 0 and n_sp % 2 == 0 and steps % group == 0
    rows, total, n_x, share = steps * cases, steps * n_tm, n_tm // 2, steps // group
    per = math.gcd(share, PER)
    chunks = share // per
    forward, inverse = tables(total, n_tm)
    own = share * 2 * cases
    state = pltpu.VMEM((own, dof), F32)
    planes_of = pltpu.VMEM((group, own, dof), F32)
    dma = pltpu.SemaphoreType.DMA
    each = [dma((group - 1, chunks)), dma((group, chunks))]
    result = pl.pallas_call(
        functools.partial(kernel, n_tm, n_sp, group, per, cases),
        out_shape=jax.ShapeDtypeStruct((rows, dof), F32),
        in_specs=[pl.BlockSpec(memory_space=pltpu.HBM)] * 8,
        out_specs=pl.BlockSpec(memory_space=pl.ANY),
        scratch_shapes=[
            pltpu.VMEM((rows, dof), BF16),
            pltpu.VMEM((rows, dof), BF16),
            pltpu.VMEM((cases, dof), BF16),
            pltpu.VMEM((dof, dof), BF16),
            pltpu.VMEM((group + 1, dof, dof), BF16),
            pltpu.VMEM((group, share, 2, dof, dof), BF16),
            pltpu.VMEM(forward.shape[1:], BF16),
            pltpu.VMEM(inverse.shape[1:], BF16),
            pltpu.VMEM((rows, dof), BF16),
            pltpu.VMEM((rows, dof), BF16),
            pltpu.VMEM((cases, dof), BF16),
            pltpu.VMEM((total * cases, dof), F32),
            pltpu.VMEM((group, dof, dof), BF16),
            planes_of, planes_of,
            pltpu.VMEM((group - 1, MARK + own, dof), BF16),
            pltpu.VMEM((group, MARK + own, dof), BF16),
            planes_of, state, state, state, planes_of,
            pltpu.VMEM((group * own, dof), F32),
            pltpu.VMEM((total * cases, dof), F32),
            pltpu.VMEM((n_x, rows, dof), F32),
            pltpu.VMEM((n_x, PIECES, rows // PIECES + MARK, dof), BF16),
            pltpu.VMEM((n_x, PIECES, rows // PIECES + MARK, dof), BF16),
            dma((8,)), dma((5,)), dma((5,)), dma((group + 1,)), dma((group + 1,)),
            dma((group - 1, share)), dma((group, share)), dma((2 * n_x,)), dma((n_tm,)), *each,
            dma((chunks,)), dma((chunks,)), dma((chunks,)), dma((chunks,)), *each,
            *[dma((n_x, PIECES))] * 4, dma((PIECES,)),
        ],
        compiler_params=pltpu.CompilerParams(
            collective_id=0, has_side_effects=True, vmem_limit_bytes=16 * 2**20
        ),
    )(
        *[
            pltpu.with_memory_space_constraint(value, pltpu.HBM)
            for value in (
                forcing.reshape(rows, dof),
                iterate.reshape(rows, dof),
                initial.reshape(cases, dof),
                stiffness.reshape(dof, dof),
                coupling.reshape(dof, dof),
                pivots.reshape(steps, 2, dof, dof),
                jnp.asarray(forward),
                jnp.asarray(inverse),
            )
        ]
    )
    return result.reshape(steps, 1, cases, dof)


def solution(mesh):
    return jax.shard_map(
        functools.partial(on_device, mesh.shape["tm"], mesh.shape["span"]),
        mesh=mesh,
        in_specs=(
            P("tm", "span", None, None),
            P("tm", "span", None, None),
            P("span", None, None),
            P("span", None, None),
            P("span", None, None),
            P("tm", "span", None, None, None),
        ),
        out_specs=P("tm", "span", None, None),
        check_vma=False,
    )
```

```python
import functools
import math

import jax
import jax.numpy as jnp
import numpy as np
from jax import lax
from jax.experimental import pallas as pl
from jax.experimental.pallas import tpu as pltpu
from jax.sharding import PartitionSpec as P

MESH = pl.DeviceIdType.MESH
F32 = jnp.float32
BF16 = jnp.bfloat16
GROUP = 4
PER = 2
LEAD = 2
PIECES = 4
CODE = 14.0
TOP = 120.0
MARK = 16


def split(value):
    high = value.astype(BF16)
    low = (value - high.astype(F32)).astype(BF16)
    return high, low


def dot(a, b):
    return jnp.dot(a, b, preferred_element_type=F32)


def encode(value, out):
    rows, lanes = value.shape
    size = jnp.maximum(jnp.abs(value), 1e-37)
    e = jnp.max(jnp.max(size, 0, keepdims=True), 1, keepdims=True)
    e = jnp.ceil(jnp.log2(jnp.maximum(e, 1e-29)))
    power = jnp.exp2(CODE * (jnp.log2(size) - e) + TOP)
    out[:MARK] = jnp.broadcast_to(e, (MARK, lanes)).astype(BF16)
    out[MARK:] = jnp.where(value < 0, -power, power).astype(BF16)


def decode(mark, power):
    power, e = power.astype(F32), mark.astype(F32)[:1]
    size = jnp.exp2((jnp.log2(jnp.maximum(jnp.abs(power), 1e-37)) - TOP) * (1.0 / CODE) + e)
    return jnp.where(power == 0, 0.0, jnp.where(power < 0, -size, size))


def tables(total, blocks):
    ids = np.arange(total)
    theta = 2.0 * math.pi / total * ((ids[:, None] * ids[None, :]) % total)
    gamma = 0.5 ** (ids / total)
    here = total // blocks

    def three(table):
        high = table.astype(np.float32).astype(jnp.bfloat16)
        low = (table - high.astype(np.float64)).astype(np.float32).astype(jnp.bfloat16)
        return np.concatenate([high, high, low], -1)

    forward = np.stack([np.cos(theta) * gamma, -np.sin(theta) * gamma], 1)
    forward = three(forward.reshape(blocks, 2 * here, total))
    back = 1.0 / (total * gamma[:, None])
    inverse = np.stack([np.cos(theta) * back, -np.sin(theta) * back], 2)
    inverse = three(inverse.reshape(total, blocks, 2 * here).transpose(1, 0, 2))
    return forward, inverse


def kernel(
    n_tm, n_sp, group, per, cases, forcing_hbm, iterate_hbm, initial_hbm, stiff_hbm, coup_hbm,
    pivots_hbm, tf_hbm, ti_hbm, out,
    forcing, iterate, initial, stiff, bonds, pivots, tf, ti,
    it_below, it_above, prior0, gath, turned, spec, spec_out, code_out, code_in, pv, q_in, q_out, x_in, solved, fin,
    contrib, rs1, sums_out, sums_in,
    ld, nb_send, nb_recv, c_send, c_recv, p_send, p_recv, ag_send, ag_recv, s_send, s_recv,
    f_send, f_recv, b_send, b_recv, e_send, e_recv, r1_send, r1_recv, r2_send, r2_recv, o_sem,
):
    tm, sp = lax.axis_index("tm"), lax.axis_index("span")
    rows, dof = iterate.shape
    steps = rows // cases
    total = steps * n_tm
    share = steps // group
    chunks = share // per
    state = 2 * cases
    size = per * state
    own_rows = share * state
    y = sp % 2
    m, g = sp % group, sp // group
    base = g * group
    n_g = n_sp // group
    n_x = n_tm // 2
    core, x = tm % 2, tm // 2
    sib = 2 * x + 1 - core
    last = n_sp - 1
    mates = [m + 1 - 2 * (m % 2)] + ([(m + 2) % 4, 3 - m] if group == 4 else [])
    has_next, has_prior = g < n_g - 1, g > 0
    pair_below, pair_above = sp > 1, sp < last - 1

    def copy(src, dst, send, recv, **where):
        return pltpu.make_async_remote_copy(
            src_ref=src, dst_ref=dst, send_sem=send, recv_sem=recv, device_id=where, device_id_type=MESH
        )

    loads = [
        pltpu.make_async_copy(src, dst, ld.at[i])
        for i, (src, dst) in enumerate(
            (
                (iterate_hbm, iterate),
                (stiff_hbm, stiff),
                (forcing_hbm, forcing),
                (initial_hbm, initial),
                (coup_hbm, bonds.at[m + 1]),
                (tf_hbm.at[tm], tf),
                (ti_hbm.at[tm], ti),
                (pivots_hbm.at[pl.ds(m * share, share)], pivots.at[m]),
            )
        )
    ]
    for load in loads:
        load.start()

    def block(b):
        return pl.ds(pl.multiple_of(b * rows, rows), rows)

    barrier = pltpu.get_barrier_semaphore()
    for i in range(1, n_tm):
        pl.semaphore_signal(barrier, inc=1, device_id={"tm": (tm + i) % n_tm}, device_id_type=MESH)
    greeted = n_tm - 1
    for d in range(1, group + 1):
        near = d in (1, 2, group)
        up_ok = sp + d <= last if near else m + d < group
        down_ok = sp >= d if near else m >= d
        for ok, there in ((up_ok, sp + d), (down_ok, sp - d)):
            @pl.when(ok)
            def _():
                pl.semaphore_signal(barrier, inc=1, device_id={"span": there}, device_id_type=MESH)

            greeted = greeted + ok.astype(jnp.int32)
    pl.semaphore_wait(barrier, greeted)

    to_up = copy(iterate_hbm, it_below, nb_send.at[0], nb_recv.at[0], span=sp + 1)
    to_down = copy(iterate_hbm, it_above, nb_send.at[1], nb_recv.at[1], span=sp - 1)
    on_up = copy(it_above, it_below, nb_send.at[2], nb_recv.at[2], span=sp + 2)
    on_down = copy(it_below, it_above, nb_send.at[3], nb_recv.at[3], span=sp - 2)
    to_next = copy(
        iterate_hbm.at[pl.ds(rows - cases, cases)], prior0, nb_send.at[4], nb_recv.at[4], tm=tm + 1
    )
    c_next = copy(coup_hbm, bonds.at[0], c_send.at[group], c_recv.at[0], span=sp + 1)
    gives_c = (m == group - 1) & has_next

    def c_copy(i):
        return copy(
            coup_hbm, bonds.at[m + 1], c_send.at[i], c_recv.at[m + 1], span=base + mates[i]
        )

    def c_wait(slot):
        copy(coup_hbm, bonds.at[slot], c_send.at[0], c_recv.at[slot], span=sp).wait_recv()

    def p_copy(i, f):
        return copy(
            pivots_hbm.at[mates[i] * share + f], pivots.at[m, f], p_send.at[i, f], p_recv.at[m, f],
            span=base + mates[i],
        )

    def p_wait(i, f):
        copy(
            pivots_hbm.at[f], pivots.at[mates[i], f], p_send.at[i, f], p_recv.at[mates[i], f],
            span=sp,
        ).wait_recv()

    def p_start(*pairs):
        for i, f in pairs:
            if i < group - 1:
                p_copy(i, f).start()

    part = [range(k * share // 4, (k + 1) * share // 4) for k in range(4)]
    late = [(i, f) for f in range(share // 2, share) for i in (1, 2)]

    @pl.when(tm < n_tm - 1)
    def _():
        to_next.start()

    @pl.when(y == 0)
    def _():
        to_up.start()

    @pl.when(y == 1)
    def _():
        to_down.start()

    for i in range(group - 1):
        c_copy(i).start()

    @pl.when(gives_c)
    def _():
        c_next.start()

    p_start(*[(i, f) for f in part[0] for i in (1, 0)])

    mine = block(tm)
    for load in loads[:5]:
        load.wait()
    it_wide = iterate[...].astype(F32)
    own = forcing[...].astype(F32) - it_wide - dot(iterate[...], stiff[...])
    own = own + jnp.concatenate([jnp.zeros((cases, dof), F32), it_wide[: rows - cases]], 0)
    gath[mine] = own
    first = pl.ds(pl.multiple_of(tm * rows, rows), cases)

    @pl.when(tm == 0)
    def _():
        gath[first] = gath[first] + initial[...].astype(F32)

    @pl.when(tm > 0)
    def _():
        to_next.wait_recv()
        gath[first] = gath[first] + prior0[...].astype(F32)

    @pl.when(y == 0)
    def _():
        to_down.wait_recv()

        @pl.when(pair_above)
        def _():
            on_up.start()

    @pl.when(y == 1)
    def _():
        to_up.wait_recv()

        @pl.when(pair_below)
        def _():
            on_down.start()

    p_start(*[(0, f) for f in part[1]], *[(2, f) for f in part[0]])

    def from_above():
        gath[mine] = gath[mine] - lax.dot_general(
            it_above[...], bonds[m + 1], (((1,), (1,)), ((), ())), preferred_element_type=F32
        )

    def from_below():
        c_wait(m)
        gath[mine] = gath[mine] - dot(it_below[...], bonds[m])

    @pl.when(y == 0)
    def _():
        from_above()

        @pl.when(pair_below)
        def _():
            on_up.wait_recv()
            from_below()

    @pl.when(y == 1)
    def _():
        from_below()

        @pl.when(pair_above)
        def _():
            on_down.wait_recv()
            from_above()

    def send_block(b, slot, peer):
        at = block(b)
        return copy(gath.at[at], gath.at[at], ag_send.at[slot], ag_recv.at[b], tm=peer)

    for i in range(1, n_x):
        send_block(tm, i, 2 * ((x + i) % n_x) + core).start()
    send_block(tm, 0, sib).start()

    p_start(*[(i, f) for f in part[1] for i in (1, 2)], *[(0, f) for f in part[2]])
    p_start(*late[:1])

    for i in range(1, group - 1):
        c_wait((m + i) % group + 1)

    @pl.when(m == 0)
    def _():
        c_wait(group)

    for p in range(group):
        turned[p] = bonds[p + 1].astype(F32).T.astype(BF16)

    @pl.when(g == 0)
    def _():
        q_in[...] = jnp.zeros_like(q_in)

    for load in loads[5:]:
        load.wait()
    for i in range(1, n_x):
        b = 2 * ((x + n_x - i) % n_x) + core
        send_block(b, 0, sib).wait_recv()
        send_block(b, n_x + i, sib).start()
    for i in range(n_x):
        send_block(2 * ((x + n_x - i) % n_x) + 1 - core, 0, sib).wait_recv()

    def at_chunk(c):
        return pl.ds(pl.multiple_of(c * size, size), size)

    def s_copy(i, c):
        start, count = (0, MARK + size) if c == 0 else (MARK + c * size, size)
        at = pl.ds(start, count)
        return copy(
            code_out.at[i, at], code_in.at[m, at], s_send.at[i, c], s_recv.at[m, c],
            span=base + mates[i],
        )

    def s_wait(i, c):
        source = mates[i]

        @pl.when(c == 0)
        def _():
            copy(
                code_out.at[i, pl.ds(0, MARK + size)], code_in.at[source, pl.ds(0, MARK + size)],
                s_send.at[i, c], s_recv.at[source, c], span=sp,
            ).wait_recv()

        at = pl.ds(pl.multiple_of(MARK + c * size, MARK), size)

        @pl.when(c > 0)
        def _():
            copy(
                code_out.at[i, at], code_in.at[source, at], s_send.at[i, c],
                s_recv.at[source, c], span=sp,
            ).wait_recv()

        spec[source, at_chunk(c)] = decode(code_in[source, :MARK], code_in[source, at])

    for case in range(0, cases, 2):
        value = jnp.concatenate(
            [gath[pl.ds(case + i, total, stride=cases), :] for i in range(2)], 1
        )
        high, low = split(value)
        result = dot(tf[...], jnp.concatenate([high, low, high], 0))
        for r in range(group):
            for i in range(2):
                spec_out[r, pl.ds(case + i, 2 * share, stride=cases), :] = result[
                    r * 2 * share : (r + 1) * 2 * share, i * dof : (i + 1) * dof
                ]
    for i in range(group - 1):
        encode(spec_out[mates[i]], code_out.at[i])
    for c in range(chunks):
        for i in range(group - 1):
            s_copy(i, c).start()
    p_start(*late[1:3], *[(0, f) for f in part[3]])
    spec[m] = spec_out[m]

    def f_copy(c):
        at = at_chunk(c)
        return copy(q_out.at[at], q_in.at[at], f_send.at[c], f_recv.at[c], span=sp + group)

    def b_copy(c):
        at = at_chunk(c)
        return copy(solved.at[0, at], x_in.at[at], b_send.at[c], b_recv.at[c], span=sp - group)

    def at_fin(q, c):
        return pl.ds(pl.multiple_of(q * own_rows + c * size, size), size)

    def e_copy(i, c):
        return copy(
            solved.at[mates[i], at_chunk(c)], fin.at[at_fin(m, c)], e_send.at[i, c],
            e_recv.at[m, c], span=base + mates[i],
        )

    def e_wait(i, c):
        copy(
            solved.at[mates[i], at_chunk(c)], fin.at[at_fin(mates[i], c)], e_send.at[i, c],
            e_recv.at[mates[i], c], span=sp,
        ).wait_recv()

    def times_pivots(value, p, c):
        high, low = split(value)
        parts = []
        for f in range(per):
            at = slice(f * state, (f + 1) * state)
            factor = jnp.concatenate([pivots[p, c * per + f, 0], pivots[p, c * per + f, 1]], 1)
            both = dot(jnp.concatenate([high[at], low[at]], 0), factor)
            both = both[:state] + both[state:]
            parts.append(both[:cases, :dof] - both[cases:, dof:])
            parts.append(both[:cases, dof:] + both[cases:, :dof])
        return jnp.concatenate(parts, 0)

    def times_bond(value, bond):
        both = dot(jnp.concatenate(split(value), 0), bond)
        return both[:size] + both[size:]

    def finish(c, at, top, lower):
        solved[group - 1, at] = top
        for p in range(group - 2, -1, -1):
            top = lower(p) - times_pivots(times_bond(top, turned[p]), p, c)
            solved[p, at] = top

        @pl.when(has_prior)
        def _():
            b_copy(c).start()

        for i in range(group - 1):
            e_copy(i, c).start()
        fin[at_fin(m, c)] = solved[m, at]

    def up(c):
        at = at_chunk(c)
        for i in range(group - 1):
            for f in range(per):
                p_wait(i, c * per + f)
            s_wait(i, c)

        @pl.when(has_prior)
        def _():
            f_copy(c).wait_recv()

        done = []
        carried = q_in[at]
        for p in range(group):
            done.append(times_pivots(spec[p, at] - carried, p, c))
            if p < group - 1:
                carried = times_bond(done[p], bonds[p + 1])

        @pl.when(has_next)
        def _():
            q_out[at] = times_bond(done[-1], bonds[group])
            f_copy(c).start()
            for p in range(group):
                pv[p, at] = done[p]

        @pl.when(g == n_g - 1)
        def _():
            finish(c, at, done[-1], lambda p: done[p])

    def down(c):
        at = at_chunk(c)
        b_copy(c).wait_recv()
        top = pv[group - 1, at] - times_pivots(
            times_bond(x_in[at], turned[group - 1]), group - 1, c
        )
        finish(c, at, top, lambda p: pv[p, at])

    lag = jnp.minimum(chunks, LEAD * (n_g - 1 - g))

    def p_more(t):
        for at, pairs in ((0, late[3:6]), (min(1, chunks - 1), late[6:])):
            @pl.when(t == at)
            def _():
                p_start(*pairs)

    def turn(t, carry):
        @pl.when(has_prior)
        def _():
            p_more(t)

        @pl.when(t < chunks)
        def _():
            up(t)

        @pl.when(g == 0)
        def _():
            p_more(t)

        @pl.when(has_next & (t >= lag) & (t < lag + chunks))
        def _():
            down(t - lag)

        return carry

    lax.fori_loop(0, 2 * chunks, turn, 0)
    for c in range(chunks):
        for i in range(group - 1):
            e_wait(i, c)

    for case in range(0, cases, 2):
        value = jnp.concatenate(
            [fin[pl.ds(case + i, 2 * steps, stride=cases), :] for i in range(2)], 1
        )
        high, low = split(value)
        result = dot(ti[...], jnp.concatenate([high, low, high], 0))
        for i in range(2):
            contrib[pl.ds(case + i, total, stride=cases), :] = result[:, i * dof : (i + 1) * dof]

    piece = rows // PIECES

    def at_piece(b, j):
        return pl.ds(pl.multiple_of(b * rows + j * piece, piece), piece)

    def r1_copy(i, j):
        there = (x + i) % n_x
        return copy(
            contrib.at[at_piece(2 * there + 1 - core, j)], rs1.at[i, pl.ds(j * piece, piece)],
            r1_send.at[i, j], r1_recv.at[i, j], tm=sib,
        )

    def r2_copy(i, j):
        return copy(
            sums_out.at[i, j], sums_in.at[i, j], r2_send.at[i, j], r2_recv.at[i, j],
            tm=2 * ((x + i) % n_x) + core,
        )

    for i in list(range(1, n_x)) + [0]:
        for j in range(PIECES):
            r1_copy(i, j).start()
    for i in range(1, n_x):
        for j in range(PIECES):
            r1_copy(i, j).wait_recv()
            at = at_piece(2 * ((x + i) % n_x) + core, j)
            encode(contrib[at] + rs1[i, pl.ds(j * piece, piece)], sums_out.at[i, j])
            r2_copy(i, j).start()
    @pl.when(tm < n_tm - 1)
    def _():
        to_next.wait_send()

    @pl.when(y == 0)
    def _():
        to_up.wait_send()

        @pl.when(pair_above)
        def _():
            on_up.wait_send()

    @pl.when(y == 1)
    def _():
        to_down.wait_send()

        @pl.when(pair_below)
        def _():
            on_down.wait_send()

    @pl.when(gives_c)
    def _():
        c_next.wait_send()

    for slot in range(2 * n_x):
        if slot != n_x:
            send_block(tm, slot, sib).wait_send()

    for i in range(group - 1):
        c_copy(i).wait_send()
        for f in range(share):
            p_copy(i, f).wait_send()
        for c in range(chunks):
            s_copy(i, c).wait_send()
            e_copy(i, c).wait_send()

    @pl.when(has_next)
    def _():
        for c in range(chunks):
            f_copy(c).wait_send()

    @pl.when(has_prior)
    def _():
        for c in range(chunks):
            b_copy(c).wait_send()

    for j in range(PIECES):
        r1_copy(0, j).wait_recv()
        own = iterate[pl.ds(j * piece, piece)].astype(F32) + rs1[0, pl.ds(j * piece, piece)]
        rs1[0, pl.ds(j * piece, piece)] = own + contrib[at_piece(tm, j)]
    for i in range(n_x):
        for j in range(PIECES):
            r1_copy(i, j).wait_send()

    def o_copy(j):
        at = pl.ds(j * piece, piece)
        return pltpu.make_async_copy(rs1.at[0, at], out.at[at], o_sem.at[j])

    for j in range(PIECES):
        result = rs1[0, pl.ds(j * piece, piece)]
        for i in range(1, n_x):
            r2_copy(i, j).wait_recv()
            result = result + decode(sums_in[i, j, :MARK], sums_in[i, j, MARK:])
        rs1[0, pl.ds(j * piece, piece)] = result
        o_copy(j).start()
    for j in range(PIECES):
        o_copy(j).wait()
        for i in range(1, n_x):
            r2_copy(i, j).wait_send()


def on_device(n_tm, n_sp, forcing, iterate, initial, stiffness, coupling, pivots):
    steps, planes, cases, dof = forcing.shape
    group = GROUP if n_sp % GROUP == 0 else 2
    assert planes == 1 and n_tm % 2 == 0 and n_sp % 2 == 0 and steps % group == 0
    rows, total, n_x, share = steps * cases, steps * n_tm, n_tm // 2, steps // group
    per = math.gcd(share, PER)
    chunks = share // per
    forward, inverse = tables(total, n_tm)
    own = share * 2 * cases
    state = pltpu.VMEM((own, dof), F32)
    planes_of = pltpu.VMEM((group, own, dof), F32)
    dma = pltpu.SemaphoreType.DMA
    each = [dma((group - 1, chunks)), dma((group, chunks))]
    result = pl.pallas_call(
        functools.partial(kernel, n_tm, n_sp, group, per, cases),
        out_shape=jax.ShapeDtypeStruct((rows, dof), F32),
        in_specs=[pl.BlockSpec(memory_space=pltpu.HBM)] * 8,
        out_specs=pl.BlockSpec(memory_space=pl.ANY),
        scratch_shapes=[
            pltpu.VMEM((rows, dof), BF16),
            pltpu.VMEM((rows, dof), BF16),
            pltpu.VMEM((cases, dof), BF16),
            pltpu.VMEM((dof, dof), BF16),
            pltpu.VMEM((group + 1, dof, dof), BF16),
            pltpu.VMEM((group, share, 2, dof, dof), BF16),
            pltpu.VMEM(forward.shape[1:], BF16),
            pltpu.VMEM(inverse.shape[1:], BF16),
            pltpu.VMEM((rows, dof), BF16),
            pltpu.VMEM((rows, dof), BF16),
            pltpu.VMEM((cases, dof), BF16),
            pltpu.VMEM((total * cases, dof), F32),
            pltpu.VMEM((group, dof, dof), BF16),
            planes_of, planes_of,
            pltpu.VMEM((group - 1, MARK + own, dof), BF16),
            pltpu.VMEM((group, MARK + own, dof), BF16),
            planes_of, state, state, state, planes_of,
            pltpu.VMEM((group * own, dof), F32),
            pltpu.VMEM((total * cases, dof), F32),
            pltpu.VMEM((n_x, rows, dof), F32),
            pltpu.VMEM((n_x, PIECES, rows // PIECES + MARK, dof), BF16),
            pltpu.VMEM((n_x, PIECES, rows // PIECES + MARK, dof), BF16),
            dma((8,)), dma((5,)), dma((5,)), dma((group + 1,)), dma((group + 1,)),
            dma((group - 1, share)), dma((group, share)), dma((2 * n_x,)), dma((n_tm,)), *each,
            dma((chunks,)), dma((chunks,)), dma((chunks,)), dma((chunks,)), *each,
            *[dma((n_x, PIECES))] * 4, dma((PIECES,)),
        ],
        compiler_params=pltpu.CompilerParams(
            collective_id=0, has_side_effects=True, vmem_limit_bytes=16 * 2**20
        ),
    )(
        *[
            pltpu.with_memory_space_constraint(value, pltpu.HBM)
            for value in (
                forcing.reshape(rows, dof),
                iterate.reshape(rows, dof),
                initial.reshape(cases, dof),
                stiffness.reshape(dof, dof),
                coupling.reshape(dof, dof),
                pivots.reshape(steps, 2, dof, dof),
                jnp.asarray(forward),
                jnp.asarray(inverse),
            )
        ]
    )
    return result.reshape(steps, 1, cases, dof)


def solution(mesh):
    return jax.shard_map(
        functools.partial(on_device, mesh.shape["tm"], mesh.shape["span"]),
        mesh=mesh,
        in_specs=(
            P("tm", "span", None, None),
            P("tm", "span", None, None),
            P("span", None, None),
            P("span", None, None),
            P("span", None, None),
            P("tm", "span", None, None, None),
        ),
        out_specs=P("tm", "span", None, None),
        check_vma=False,
    )
```

```python
import functools
import math

import jax
import jax.numpy as jnp
import numpy as np
from jax import lax
from jax.experimental import pallas as pl
from jax.experimental.pallas import tpu as pltpu
from jax.sharding import PartitionSpec as P

MESH = pl.DeviceIdType.MESH
F32 = jnp.float32
BF16 = jnp.bfloat16
GROUP = 4
PER = 2
LEAD = 3
PIECES = 2
CODE = 14.0
TOP = 120.0
MARK = 16


def split(value):
    high = value.astype(BF16)
    low = (value - high.astype(F32)).astype(BF16)
    return high, low


def dot(a, b):
    return jnp.dot(a, b, preferred_element_type=F32)


def encode(value, out):
    rows, lanes = value.shape
    size = jnp.maximum(jnp.abs(value), 1e-37)
    e = jnp.max(jnp.max(size, 0, keepdims=True), 1, keepdims=True)
    e = jnp.ceil(jnp.log2(jnp.maximum(e, 1e-29)))
    power = jnp.exp2(CODE * (jnp.log2(size) - e) + TOP)
    out[:MARK] = jnp.broadcast_to(e, (MARK, lanes)).astype(BF16)
    out[MARK:] = jnp.where(value < 0, -power, power).astype(BF16)


def decode(mark, power):
    power, e = power.astype(F32), mark.astype(F32)[:1]
    size = jnp.exp2((jnp.log2(jnp.maximum(jnp.abs(power), 1e-37)) - TOP) * (1.0 / CODE) + e)
    return jnp.where(power == 0, 0.0, jnp.where(power < 0, -size, size))


def tables(total, blocks):
    ids = np.arange(total)
    theta = 2.0 * math.pi / total * ((ids[:, None] * ids[None, :]) % total)
    gamma = 0.5 ** (ids / total)
    here = total // blocks

    def three(table):
        high = table.astype(np.float32).astype(jnp.bfloat16)
        low = (table - high.astype(np.float64)).astype(np.float32).astype(jnp.bfloat16)
        return np.concatenate([high, high, low], -1)

    forward = np.stack([np.cos(theta) * gamma, -np.sin(theta) * gamma], 1)
    forward = three(forward.reshape(blocks, 2 * here, total))
    back = 1.0 / (total * gamma[:, None])
    inverse = np.stack([np.cos(theta) * back, -np.sin(theta) * back], 2)
    inverse = three(inverse.reshape(total, blocks, 2 * here).transpose(1, 0, 2))
    return forward, inverse


def kernel(
    n_tm, n_sp, group, per, cases, forcing_hbm, iterate_hbm, initial_hbm, stiff_hbm, coup_hbm,
    pivots_hbm, tf_hbm, ti_hbm, out,
    forcing, iterate, initial, stiff, bonds, pivots, tf, ti,
    it_below, it_above, prior0, gath, turned, spec, spec_out, code_out, code_in, pv, q_in, q_out, x_in, solved, fin,
    contrib, rs1, sums_out, sums_in,
    ld, nb_send, nb_recv, c_send, c_recv, p_send, p_recv, ag_send, ag_recv, s_send, s_recv,
    f_send, f_recv, b_send, b_recv, e_send, e_recv, r1_send, r1_recv, r2_send, r2_recv, o_sem,
):
    tm, sp = lax.axis_index("tm"), lax.axis_index("span")
    rows, dof = iterate.shape
    steps = rows // cases
    total = steps * n_tm
    share = steps // group
    chunks = share // per
    state = 2 * cases
    size = per * state
    own_rows = share * state
    y = sp % 2
    m, g = sp % group, sp // group
    base = g * group
    n_g = n_sp // group
    n_x = n_tm // 2
    core, x = tm % 2, tm // 2
    sib = 2 * x + 1 - core
    last = n_sp - 1
    mates = [m + 1 - 2 * (m % 2)] + ([(m + 2) % 4, 3 - m] if group == 4 else [])
    has_next, has_prior = g < n_g - 1, g > 0
    pair_below, pair_above = sp > 1, sp < last - 1

    def copy(src, dst, send, recv, **where):
        return pltpu.make_async_remote_copy(
            src_ref=src, dst_ref=dst, send_sem=send, recv_sem=recv, device_id=where, device_id_type=MESH
        )

    loads = [
        pltpu.make_async_copy(src, dst, ld.at[i])
        for i, (src, dst) in enumerate(
            (
                (iterate_hbm, iterate),
                (stiff_hbm, stiff),
                (forcing_hbm, forcing),
                (initial_hbm, initial),
                (coup_hbm, bonds.at[m + 1]),
                (tf_hbm.at[tm], tf),
                (ti_hbm.at[tm], ti),
                (pivots_hbm.at[pl.ds(m * share, share)], pivots.at[m]),
            )
        )
    ]
    for load in loads:
        load.start()

    def block(b):
        return pl.ds(pl.multiple_of(b * rows, rows), rows)

    barrier = pltpu.get_barrier_semaphore()
    for i in range(1, n_tm):
        pl.semaphore_signal(barrier, inc=1, device_id={"tm": (tm + i) % n_tm}, device_id_type=MESH)
    greeted = n_tm - 1
    for d in range(1, group + 1):
        near = d in (1, 2, group)
        up_ok = sp + d <= last if near else m + d < group
        down_ok = sp >= d if near else m >= d
        for ok, there in ((up_ok, sp + d), (down_ok, sp - d)):
            @pl.when(ok)
            def _():
                pl.semaphore_signal(barrier, inc=1, device_id={"span": there}, device_id_type=MESH)

            greeted = greeted + ok.astype(jnp.int32)
    pl.semaphore_wait(barrier, greeted)

    to_up = copy(iterate_hbm, it_below, nb_send.at[0], nb_recv.at[0], span=sp + 1)
    to_down = copy(iterate_hbm, it_above, nb_send.at[1], nb_recv.at[1], span=sp - 1)
    on_up = copy(it_above, it_below, nb_send.at[2], nb_recv.at[2], span=sp + 2)
    on_down = copy(it_below, it_above, nb_send.at[3], nb_recv.at[3], span=sp - 2)
    to_next = copy(
        iterate_hbm.at[pl.ds(rows - cases, cases)], prior0, nb_send.at[4], nb_recv.at[4], tm=tm + 1
    )
    c_next = copy(coup_hbm, bonds.at[0], c_send.at[group], c_recv.at[0], span=sp + 1)
    gives_c = (m == group - 1) & has_next

    def c_copy(i):
        return copy(
            coup_hbm, bonds.at[m + 1], c_send.at[i], c_recv.at[m + 1], span=base + mates[i]
        )

    def c_wait(slot):
        copy(coup_hbm, bonds.at[slot], c_send.at[0], c_recv.at[slot], span=sp).wait_recv()

    def p_copy(i, f):
        return copy(
            pivots_hbm.at[mates[i] * share + f], pivots.at[m, f], p_send.at[i, f], p_recv.at[m, f],
            span=base + mates[i],
        )

    def p_wait(i, f):
        copy(
            pivots_hbm.at[f], pivots.at[mates[i], f], p_send.at[i, f], p_recv.at[mates[i], f],
            span=sp,
        ).wait_recv()

    def p_start(*pairs):
        for i, f in pairs:
            if i < group - 1:
                p_copy(i, f).start()

    part = [range(k * share // 4, (k + 1) * share // 4) for k in range(4)]
    late = [(i, f) for f in range(share // 2, share) for i in (1, 2)]

    @pl.when(tm < n_tm - 1)
    def _():
        to_next.start()

    @pl.when(y == 0)
    def _():
        to_up.start()

    @pl.when(y == 1)
    def _():
        to_down.start()

    for i in range(group - 1):
        c_copy(i).start()

    @pl.when(gives_c)
    def _():
        c_next.start()

    p_start(*[(i, f) for f in part[0] for i in (1, 0)])

    mine = block(tm)
    for load in loads[:5]:
        load.wait()
    it_wide = iterate[...].astype(F32)
    own = forcing[...].astype(F32) - it_wide - dot(iterate[...], stiff[...])
    own = own + jnp.concatenate([jnp.zeros((cases, dof), F32), it_wide[: rows - cases]], 0)
    gath[mine] = own
    first = pl.ds(pl.multiple_of(tm * rows, rows), cases)

    @pl.when(tm == 0)
    def _():
        gath[first] = gath[first] + initial[...].astype(F32)

    @pl.when(tm > 0)
    def _():
        to_next.wait_recv()
        gath[first] = gath[first] + prior0[...].astype(F32)

    @pl.when(y == 0)
    def _():
        to_down.wait_recv()

        @pl.when(pair_above)
        def _():
            on_up.start()

    @pl.when(y == 1)
    def _():
        to_up.wait_recv()

        @pl.when(pair_below)
        def _():
            on_down.start()

    p_start(*[(0, f) for f in part[1]], *[(2, f) for f in part[0]])

    def from_above():
        gath[mine] = gath[mine] - lax.dot_general(
            it_above[...], bonds[m + 1], (((1,), (1,)), ((), ())), preferred_element_type=F32
        )

    def from_below():
        c_wait(m)
        gath[mine] = gath[mine] - dot(it_below[...], bonds[m])

    @pl.when(y == 0)
    def _():
        from_above()

        @pl.when(pair_below)
        def _():
            on_up.wait_recv()
            from_below()

    @pl.when(y == 1)
    def _():
        from_below()

        @pl.when(pair_above)
        def _():
            on_down.wait_recv()
            from_above()

    def send_block(b, slot, peer):
        at = block(b)
        return copy(gath.at[at], gath.at[at], ag_send.at[slot], ag_recv.at[b], tm=peer)

    for i in range(1, n_x):
        send_block(tm, i, 2 * ((x + i) % n_x) + core).start()
    send_block(tm, 0, sib).start()

    p_start(*[(i, f) for f in part[1] for i in (1, 2)], *[(0, f) for f in part[2]])
    p_start(*late[:1])

    for i in range(1, group - 1):
        c_wait((m + i) % group + 1)

    @pl.when(m == 0)
    def _():
        c_wait(group)

    for p in range(group):
        turned[p] = bonds[p + 1].astype(F32).T.astype(BF16)

    @pl.when(g == 0)
    def _():
        q_in[...] = jnp.zeros_like(q_in)

    for load in loads[5:]:
        load.wait()
    for i in range(1, n_x):
        b = 2 * ((x + n_x - i) % n_x) + core
        send_block(b, 0, sib).wait_recv()
        send_block(b, n_x + i, sib).start()
    for i in range(n_x):
        send_block(2 * ((x + n_x - i) % n_x) + 1 - core, 0, sib).wait_recv()

    def at_chunk(c):
        return pl.ds(pl.multiple_of(c * size, size), size)

    def s_copy(i, c):
        start, count = (0, MARK + size) if c == 0 else (MARK + c * size, size)
        at = pl.ds(start, count)
        return copy(
            code_out.at[i, at], code_in.at[m, at], s_send.at[i, c], s_recv.at[m, c],
            span=base + mates[i],
        )

    def s_wait(i, c):
        source = mates[i]

        @pl.when(c == 0)
        def _():
            copy(
                code_out.at[i, pl.ds(0, MARK + size)], code_in.at[source, pl.ds(0, MARK + size)],
                s_send.at[i, c], s_recv.at[source, c], span=sp,
            ).wait_recv()

        at = pl.ds(pl.multiple_of(MARK + c * size, MARK), size)

        @pl.when(c > 0)
        def _():
            copy(
                code_out.at[i, at], code_in.at[source, at], s_send.at[i, c],
                s_recv.at[source, c], span=sp,
            ).wait_recv()

        spec[source, at_chunk(c)] = decode(code_in[source, :MARK], code_in[source, at])

    for case in range(0, cases, 2):
        value = jnp.concatenate(
            [gath[pl.ds(case + i, total, stride=cases), :] for i in range(2)], 1
        )
        high, low = split(value)
        result = dot(tf[...], jnp.concatenate([high, low, high], 0))
        for r in range(group):
            for i in range(2):
                spec_out[r, pl.ds(case + i, 2 * share, stride=cases), :] = result[
                    r * 2 * share : (r + 1) * 2 * share, i * dof : (i + 1) * dof
                ]
    for i in range(group - 1):
        encode(spec_out[mates[i]], code_out.at[i])
    for c in range(chunks):
        for i in range(group - 1):
            s_copy(i, c).start()
    p_start(*late[1:3], *[(0, f) for f in part[3]])
    spec[m] = spec_out[m]

    def f_copy(c):
        at = at_chunk(c)
        return copy(q_out.at[at], q_in.at[at], f_send.at[c], f_recv.at[c], span=sp + group)

    def b_copy(c):
        at = at_chunk(c)
        return copy(solved.at[0, at], x_in.at[at], b_send.at[c], b_recv.at[c], span=sp - group)

    def at_fin(q, c):
        return pl.ds(pl.multiple_of(q * own_rows + c * size, size), size)

    def e_copy(i, c):
        return copy(
            solved.at[mates[i], at_chunk(c)], fin.at[at_fin(m, c)], e_send.at[i, c],
            e_recv.at[m, c], span=base + mates[i],
        )

    def e_wait(i, c):
        copy(
            solved.at[mates[i], at_chunk(c)], fin.at[at_fin(mates[i], c)], e_send.at[i, c],
            e_recv.at[mates[i], c], span=sp,
        ).wait_recv()

    def times_pivots(value, p, c):
        high, low = split(value)
        parts = []
        for f in range(per):
            at = slice(f * state, (f + 1) * state)
            factor = jnp.concatenate([pivots[p, c * per + f, 0], pivots[p, c * per + f, 1]], 1)
            both = dot(jnp.concatenate([high[at], low[at]], 0), factor)
            both = both[:state] + both[state:]
            parts.append(both[:cases, :dof] - both[cases:, dof:])
            parts.append(both[:cases, dof:] + both[cases:, :dof])
        return jnp.concatenate(parts, 0)

    def times_bond(value, bond):
        both = dot(jnp.concatenate(split(value), 0), bond)
        return both[:size] + both[size:]

    def finish(c, at, top, lower):
        solved[group - 1, at] = top
        for p in range(group - 2, -1, -1):
            top = lower(p) - times_pivots(times_bond(top, turned[p]), p, c)
            solved[p, at] = top

        @pl.when(has_prior)
        def _():
            b_copy(c).start()

        for i in range(group - 1):
            e_copy(i, c).start()
        fin[at_fin(m, c)] = solved[m, at]

    def up(c):
        at = at_chunk(c)
        for i in range(group - 1):
            for f in range(per):
                p_wait(i, c * per + f)
            s_wait(i, c)

        @pl.when(has_prior)
        def _():
            f_copy(c).wait_recv()

        done = []
        carried = q_in[at]
        for p in range(group):
            done.append(times_pivots(spec[p, at] - carried, p, c))
            if p < group - 1:
                carried = times_bond(done[p], bonds[p + 1])

        @pl.when(has_next)
        def _():
            q_out[at] = times_bond(done[-1], bonds[group])
            f_copy(c).start()
            for p in range(group):
                pv[p, at] = done[p]

        @pl.when(g == n_g - 1)
        def _():
            finish(c, at, done[-1], lambda p: done[p])

    def down(c):
        at = at_chunk(c)
        b_copy(c).wait_recv()
        top = pv[group - 1, at] - times_pivots(
            times_bond(x_in[at], turned[group - 1]), group - 1, c
        )
        finish(c, at, top, lambda p: pv[p, at])

    lag = jnp.minimum(chunks, LEAD * (n_g - 1 - g))

    def p_more(t):
        for at, pairs in ((0, late[3:7]), (min(1, chunks - 1), late[7:])):
            @pl.when(t == at)
            def _():
                p_start(*pairs)

    def turn(t, carry):
        @pl.when(has_prior)
        def _():
            p_more(t)

        @pl.when(t < chunks)
        def _():
            up(t)

        @pl.when(g == 0)
        def _():
            p_more(t)

        @pl.when(has_next & (t >= lag) & (t < lag + chunks))
        def _():
            down(t - lag)

        return carry

    lax.fori_loop(0, 2 * chunks, turn, 0)
    for c in range(chunks):
        for i in range(group - 1):
            e_wait(i, c)

    for case in range(0, cases, 2):
        value = jnp.concatenate(
            [fin[pl.ds(case + i, 2 * steps, stride=cases), :] for i in range(2)], 1
        )
        high, low = split(value)
        result = dot(ti[...], jnp.concatenate([high, low, high], 0))
        for i in range(2):
            contrib[pl.ds(case + i, total, stride=cases), :] = result[:, i * dof : (i + 1) * dof]

    piece = rows // PIECES

    def at_piece(b, j):
        return pl.ds(pl.multiple_of(b * rows + j * piece, piece), piece)

    def r1_copy(i, j):
        there = (x + i) % n_x
        return copy(
            contrib.at[at_piece(2 * there + 1 - core, j)], rs1.at[i, pl.ds(j * piece, piece)],
            r1_send.at[i, j], r1_recv.at[i, j], tm=sib,
        )

    def r2_copy(i, j):
        return copy(
            sums_out.at[i, j], sums_in.at[i, j], r2_send.at[i, j], r2_recv.at[i, j],
            tm=2 * ((x + i) % n_x) + core,
        )

    for i in list(range(1, n_x)) + [0]:
        for j in range(PIECES):
            r1_copy(i, j).start()
    for i in range(1, n_x):
        for j in range(PIECES):
            r1_copy(i, j).wait_recv()
            at = at_piece(2 * ((x + i) % n_x) + core, j)
            encode(contrib[at] + rs1[i, pl.ds(j * piece, piece)], sums_out.at[i, j])
            r2_copy(i, j).start()
    @pl.when(tm < n_tm - 1)
    def _():
        to_next.wait_send()

    @pl.when(y == 0)
    def _():
        to_up.wait_send()

        @pl.when(pair_above)
        def _():
            on_up.wait_send()

    @pl.when(y == 1)
    def _():
        to_down.wait_send()

        @pl.when(pair_below)
        def _():
            on_down.wait_send()

    @pl.when(gives_c)
    def _():
        c_next.wait_send()

    for slot in range(2 * n_x):
        if slot != n_x:
            send_block(tm, slot, sib).wait_send()

    for i in range(group - 1):
        c_copy(i).wait_send()
        for f in range(share):
            p_copy(i, f).wait_send()
        for c in range(chunks):
            s_copy(i, c).wait_send()
            e_copy(i, c).wait_send()

    @pl.when(has_next)
    def _():
        for c in range(chunks):
            f_copy(c).wait_send()

    @pl.when(has_prior)
    def _():
        for c in range(chunks):
            b_copy(c).wait_send()

    for j in range(PIECES):
        r1_copy(0, j).wait_recv()
        own = iterate[pl.ds(j * piece, piece)].astype(F32) + rs1[0, pl.ds(j * piece, piece)]
        rs1[0, pl.ds(j * piece, piece)] = own + contrib[at_piece(tm, j)]
    for i in range(n_x):
        for j in range(PIECES):
            r1_copy(i, j).wait_send()

    def o_copy(j):
        at = pl.ds(j * piece, piece)
        return pltpu.make_async_copy(rs1.at[0, at], out.at[at], o_sem.at[j])

    for j in range(PIECES):
        result = rs1[0, pl.ds(j * piece, piece)]
        for i in range(1, n_x):
            r2_copy(i, j).wait_recv()
            result = result + decode(sums_in[i, j, :MARK], sums_in[i, j, MARK:])
        rs1[0, pl.ds(j * piece, piece)] = result
        o_copy(j).start()
    for j in range(PIECES):
        o_copy(j).wait()
        for i in range(1, n_x):
            r2_copy(i, j).wait_send()


def on_device(n_tm, n_sp, forcing, iterate, initial, stiffness, coupling, pivots):
    steps, planes, cases, dof = forcing.shape
    group = GROUP if n_sp % GROUP == 0 else 2
    assert planes == 1 and n_tm % 2 == 0 and n_sp % 2 == 0 and steps % group == 0
    rows, total, n_x, share = steps * cases, steps * n_tm, n_tm // 2, steps // group
    per = math.gcd(share, PER)
    chunks = share // per
    forward, inverse = tables(total, n_tm)
    own = share * 2 * cases
    state = pltpu.VMEM((own, dof), F32)
    planes_of = pltpu.VMEM((group, own, dof), F32)
    dma = pltpu.SemaphoreType.DMA
    each = [dma((group - 1, chunks)), dma((group, chunks))]
    result = pl.pallas_call(
        functools.partial(kernel, n_tm, n_sp, group, per, cases),
        out_shape=jax.ShapeDtypeStruct((rows, dof), F32),
        in_specs=[pl.BlockSpec(memory_space=pltpu.HBM)] * 8,
        out_specs=pl.BlockSpec(memory_space=pl.ANY),
        scratch_shapes=[
            pltpu.VMEM((rows, dof), BF16),
            pltpu.VMEM((rows, dof), BF16),
            pltpu.VMEM((cases, dof), BF16),
            pltpu.VMEM((dof, dof), BF16),
            pltpu.VMEM((group + 1, dof, dof), BF16),
            pltpu.VMEM((group, share, 2, dof, dof), BF16),
            pltpu.VMEM(forward.shape[1:], BF16),
            pltpu.VMEM(inverse.shape[1:], BF16),
            pltpu.VMEM((rows, dof), BF16),
            pltpu.VMEM((rows, dof), BF16),
            pltpu.VMEM((cases, dof), BF16),
            pltpu.VMEM((total * cases, dof), F32),
            pltpu.VMEM((group, dof, dof), BF16),
            planes_of, planes_of,
            pltpu.VMEM((group - 1, MARK + own, dof), BF16),
            pltpu.VMEM((group, MARK + own, dof), BF16),
            planes_of, state, state, state, planes_of,
            pltpu.VMEM((group * own, dof), F32),
            pltpu.VMEM((total * cases, dof), F32),
            pltpu.VMEM((n_x, rows, dof), F32),
            pltpu.VMEM((n_x, PIECES, rows // PIECES + MARK, dof), BF16),
            pltpu.VMEM((n_x, PIECES, rows // PIECES + MARK, dof), BF16),
            dma((8,)), dma((5,)), dma((5,)), dma((group + 1,)), dma((group + 1,)),
            dma((group - 1, share)), dma((group, share)), dma((2 * n_x,)), dma((n_tm,)), *each,
            dma((chunks,)), dma((chunks,)), dma((chunks,)), dma((chunks,)), *each,
            *[dma((n_x, PIECES))] * 4, dma((PIECES,)),
        ],
        compiler_params=pltpu.CompilerParams(
            collective_id=0, has_side_effects=True, vmem_limit_bytes=16 * 2**20
        ),
    )(
        *[
            pltpu.with_memory_space_constraint(value, pltpu.HBM)
            for value in (
                forcing.reshape(rows, dof),
                iterate.reshape(rows, dof),
                initial.reshape(cases, dof),
                stiffness.reshape(dof, dof),
                coupling.reshape(dof, dof),
                pivots.reshape(steps, 2, dof, dof),
                jnp.asarray(forward),
                jnp.asarray(inverse),
            )
        ]
    )
    return result.reshape(steps, 1, cases, dof)


def solution(mesh):
    return jax.shard_map(
        functools.partial(on_device, mesh.shape["tm"], mesh.shape["span"]),
        mesh=mesh,
        in_specs=(
            P("tm", "span", None, None),
            P("tm", "span", None, None),
            P("span", None, None),
            P("span", None, None),
            P("span", None, None),
            P("tm", "span", None, None, None),
        ),
        out_specs=P("tm", "span", None, None),
        check_vma=False,
    )
```
